1024 devices in a mesh: energy: 64 (over y, x), slab: 16 (over z, core).
Axes of the slice: x: 8, y: 8, z: 8, core: 2. Of those that a mesh axis runs over, the one named last changes fastest.
Arguments:
- green_local: bfloat16 [64, 6144, 768], P('energy', 'slab'), may hold values from -6 to 6
- coupling: bfloat16 [6144, 384], P('slab'), may hold values from -0.3125 to 0.3125
- phonon_coupling: bfloat16 [3, 384, 384], replicated, may hold values from -0.3125 to 0.3125
- offsets: int32 [3], replicated, may hold values from 1 to 4, as said below
- bose_factors: float32 [3], replicated, may hold values from 0.2 to 3
Outputs:
- phonon_sigma: bfloat16 [64, 6144, 768], P('energy', 'slab')
- cumulative: float32 [64, 6144], P('energy', 'slab')
The draws below stay inside these ranges and needn't reach their ends.
Inputs may be any that keep to these rules, and one draw needn't show every extreme that they name: The offsets are distinct, and one of them equals 4.
All inputs are finite; a program needn't handle non-finite values.
Results may differ from the reference program's by a relative error of at most 0.018.
Values may be sent and summed in bfloat16 or wider, within the bound.
A program may use at most 32 MiB of HBM per device.

```python
import math
import jax
import jax.numpy as jnp
from jax import lax

M = 384
MODES = 3
OMAX = 4
ENERGIES = 64
SLABS = 16


def draw_offsets(key, part):
    key_one, key_two = jax.random.split(jax.random.fold_in(key, 7))
    smaller = jax.random.permutation(key_one, OMAX - 1) + 1
    chosen = jnp.concatenate([smaller[:MODES - 1], jnp.array([OMAX])])
    return jax.random.permutation(key_two, chosen).astype(jnp.int32)


def level_of(own_key, shape, cuts, smallest, largest):
    def one(position, blocks):
        draws = jax.random.uniform(jax.random.fold_in(jax.random.fold_in(own_key, 6), position), (blocks,), jnp.float32, smallest / len(cuts), largest / len(cuts))
        return jnp.repeat(jnp.exp(draws), shape[position] // blocks).reshape((-1,) + (1,) * (len(shape) - position - 1))

    loudness = one(*cuts[0])
    for cut in cuts[1:]:
        loudness = loudness * one(*cut)
    return loudness


def centred(own_key, shape, spread, bound, pieces=(), kind=jnp.bfloat16):
    result = spread * jax.random.normal(own_key, shape, jnp.float32)
    if pieces:
        result = result * level_of(own_key, shape, pieces, -0.22, 0.18)
    return jnp.clip(result, -bound, bound).astype(kind)


def setup_inputs(seed: int = 0) -> dict:
    seeds = jax.random.split(jax.random.key(seed), 6)
    green_local = centred(seeds[0], (ENERGIES, SLABS * M, 2 * M), 1.0, 6.0, ((0, 64), (1, 16)))
    coupling = centred(seeds[1], (SLABS * M, M), M ** -0.5, 0.3125, ((0, 16),))
    phonon_coupling = centred(seeds[2], (MODES, M, M), M ** -0.5, 0.3125)
    offsets = draw_offsets(jax.random.fold_in(seeds[5], 71), 0)
    bose_factors = jnp.clip(jnp.exp(jax.random.uniform(seeds[4], (MODES,), jnp.float32, math.log(0.2), math.log(3.0))), 0.2, 3.0)
    return dict(green_local=green_local, coupling=coupling, phonon_coupling=phonon_coupling, offsets=offsets, bose_factors=bose_factors)


def left_real(matrices, blocks):
    return jnp.einsum('eab,ebc->eac', matrices.astype(jnp.float32), blocks.astype(jnp.float32))


def right_real(blocks, matrices):
    batch_size, row_count, double = blocks.shape
    halves = blocks.reshape(batch_size, row_count, 2, double // 2).astype(jnp.float32)
    product = jnp.einsum('eatm,emb->eatb', halves, matrices.astype(jnp.float32))
    return product.reshape(batch_size, row_count, double)


def complex_matrix(blocks):
    half_width = blocks.shape[-1] // 2
    real_part = blocks[..., :half_width]
    imag_part = blocks[..., half_width:]
    top_rows = jnp.concatenate([real_part, imag_part], axis=-1)
    bottom_rows = jnp.concatenate([-imag_part, real_part], axis=-1)
    return jnp.concatenate([top_rows, bottom_rows], axis=-2)


def complex_product(first, second):
    return jnp.einsum('eam,emn->ean', first.astype(jnp.float32), complex_matrix(second).astype(jnp.float32))


def reference(green_local, coupling, phonon_coupling, offsets, bose_factors):
    energies = green_local.shape[0]
    blocks = green_local.reshape(energies, SLABS, M, 2 * M)
    links = coupling.reshape(SLABS, M, M)
    links_transposed = jnp.swapaxes(links, 1, 2)
    zero_link = jnp.zeros((1, M, M), jnp.bfloat16)
    lower_links = jnp.concatenate([zero_link, links[:-1]], axis=0)
    lower_transposed = jnp.swapaxes(lower_links, 1, 2)

    def dress(energy_blocks):
        zero_block = jnp.zeros((1, M, 2 * M), jnp.bfloat16)
        upper_blocks = jnp.concatenate([energy_blocks[1:], zero_block], axis=0)
        lower_blocks = jnp.concatenate([zero_block, energy_blocks[:-1]], axis=0)
        up_left = left_real(links, upper_blocks).astype(jnp.bfloat16)
        upper_term = right_real(up_left, links_transposed).astype(jnp.bfloat16)
        down_left = left_real(lower_transposed, lower_blocks).astype(jnp.bfloat16)
        lower_term = right_real(down_left, lower_links).astype(jnp.bfloat16)
        couple = (upper_term.astype(jnp.float32) + lower_term.astype(jnp.float32)).astype(jnp.bfloat16)
        dressed = complex_product(energy_blocks, couple).astype(jnp.bfloat16)
        corrected = energy_blocks.astype(jnp.float32) + complex_product(dressed, energy_blocks) / M
        return corrected.astype(jnp.bfloat16)

    greens = lax.map(dress, blocks)

    positions = jnp.arange(energies, dtype=jnp.int32).astype(jnp.float32)
    holes = jax.nn.sigmoid((positions + 0.5 - energies / 2) * 4.0 / energies)
    imag_diag = jnp.diagonal(greens[..., M:], axis1=2, axis2=3).astype(jnp.float32)
    dos_terms = -holes[:, None, None] * imag_diag
    cumulative = jnp.cumsum(dos_terms, axis=0).reshape(energies, SLABS * M)

    phonon_transposed = jnp.swapaxes(phonon_coupling, 1, 2)

    def self_energy(energy):
        accumulated = jnp.zeros((SLABS, M, 2 * M), jnp.float32)
        for mode_index in range(MODES):
            shift_size = offsets[mode_index]
            below_index = energy - shift_size
            above_index = energy + shift_size
            lower_block = greens[jnp.clip(below_index, 0, energies - 1)].astype(jnp.float32) * (below_index >= 0).astype(jnp.float32)
            upper_block = greens[jnp.clip(above_index, 0, energies - 1)].astype(jnp.float32) * (above_index < energies).astype(jnp.float32)
            factor = bose_factors[mode_index]
            mixture = ((factor + 1.0) * lower_block + factor * upper_block).astype(jnp.bfloat16)
            matrices = jnp.broadcast_to(phonon_coupling[mode_index][None], (SLABS, M, M))
            matrices_transposed = jnp.broadcast_to(phonon_transposed[mode_index][None], (SLABS, M, M))
            phonon_left = left_real(matrices, mixture).astype(jnp.bfloat16)
            accumulated = accumulated + right_real(phonon_left, matrices_transposed)
        return accumulated.astype(jnp.bfloat16)

    phonon_sigma = lax.map(self_energy, jnp.arange(energies, dtype=jnp.int32))
    phonon_sigma = phonon_sigma.reshape(energies, SLABS * M, 2 * M)
    return phonon_sigma, cumulative
```

```python
import functools

import jax
import jax.numpy as jnp
from jax import lax
from jax.experimental import pallas as pl
from jax.experimental.pallas import tpu as pltpu
from jax.sharding import PartitionSpec as P

M = 384
MODES = 3
ROW = 8
CHUNKS = 2
ROWS = M // CHUNKS
MESH = pl.DeviceIdType.MESH
F32 = jnp.float32
BF16 = jnp.bfloat16

ROUTES = {
    (1, 2, 3, 4): {
        "right": [(0, 0, 1), (0, 1, 2), (0, 2, 3), (0, 3, 4), (1, 0, 1), (1, 1, 2), (1, 2, 3)],
        "down": [(0, 4, -4)],
    },
}


def slot_of(offset):
    return offset + 4 if offset < 0 else offset + 3


def plan(distances, chunk_us=3.2, latency_us=1.6):
    base = ROUTES[distances]
    links = {
        "right": base["right"],
        "left": [(1 - h, -a, -b) for h, a, b in base["right"]],
        "down": base["down"],
        "up": [(1 - h, -a, -b) for h, a, b in base["down"]],
    }
    ready = {(h, 0, c): 0.8 * c for h in range(2) for c in range(CHUNKS)}
    queues = {name: [(h, a, b, c) for h, a, b in routes for c in range(CHUNKS)] for name, routes in links.items()}
    free = {name: 0.0 for name in links}
    last = {name: 0.0 for name in links}
    events = []
    while any(queues.values()):
        for name, queue in queues.items():
            while queue and (queue[0][0], queue[0][1], queue[0][3]) in ready:
                h, a, b, c = queue.pop(0)
                source = ready[(h, a, c)]
                last[name] = max(last[name], source)
                free[name] = max(free[name], source) + chunk_us
                ready[(h, b, c)] = free[name] + latency_us
                events.append((last[name], 0, ("send", h, a, b, c)))
    for d in distances:
        for h in range(2):
            when = max(ready[(h, o, c)] for o in (-d, d) for c in range(CHUNKS))
            events.append((when, 1, ("product", d, h)))
    after = max(ready[(0, 1, c)] for c in range(CHUNKS))
    for order, name in enumerate(("sum4", "sum8", "sum32", "sum64")):
        events.append((after + 6.4 * order, 2, (name,)))
    events.sort(key=lambda event: event[:2])
    return [event[2] for event in events]


def mm(a, b):
    return jnp.dot(a, b, preferred_element_type=F32)


def kernel(
    distances, energies, slabs,
    g_hbm, b_hbm, p_hbm, off_ref, bose_ref,
    sigma_ref, cum_ref,
    gv, bv, bt, pv, pt, gup, low_in, low_out, couple, greens, slots, acc,
    own_sum, own4, own8, own32, got1, got4, got8, got32,
    load_sem, zsend, zrecv, hsend, hrecv, ssend, srecv, tokens,
):
    e = lax.axis_index("energy")
    s = lax.axis_index("slab")
    first = s == 0
    last = s == slabs - 1

    def at(step):
        return lax.rem(e + (step + energies), energies)

    near = (1, -1, ROW, -ROW)
    barrier = pltpu.get_barrier_semaphore()
    for step in near:
        pl.semaphore_signal(barrier, inc=1, device_id=(at(step), s), device_id_type=MESH)

    @pl.when(s > 0)
    def _():
        pl.semaphore_signal(barrier, inc=1, device_id=(e, s - 1), device_id_type=MESH)

    @pl.when(s < slabs - 1)
    def _():
        pl.semaphore_signal(barrier, inc=1, device_id=(e, s + 1), device_id_type=MESH)

    loads = [
        pltpu.make_async_copy(g_hbm.at[0, :, pl.ds(0, M)], gv.at[0], load_sem.at[0]),
        pltpu.make_async_copy(b_hbm, bv, load_sem.at[1]),
        pltpu.make_async_copy(g_hbm.at[0, :, pl.ds(M, M)], gv.at[1], load_sem.at[2]),
        pltpu.make_async_copy(p_hbm, pv, load_sem.at[3]),
    ]
    for load in loads:
        load.start()

    slab_links = jnp.where(first, 0, 1) + jnp.where(last, 0, 1)
    pl.semaphore_wait(barrier, len(near) + slab_links)

    downs = [
        pltpu.make_async_remote_copy(
            src_ref=g_hbm.at[0, :, pl.ds(h * M, M)], dst_ref=gup.at[h],
            send_sem=zsend.at[h], recv_sem=zrecv.at[h],
            device_id=(e, s - 1), device_id_type=MESH)
        for h in range(2)
    ]
    ups = [
        pltpu.make_async_remote_copy(
            src_ref=low_out.at[h], dst_ref=low_in.at[h],
            send_sem=zsend.at[2 + h], recv_sem=zrecv.at[2 + h],
            device_id=(e, s + 1), device_id_type=MESH)
        for h in range(2)
    ]

    @pl.when(s > 0)
    def _():
        for copy in downs:
            copy.start()

    def token(index):
        for step in near:
            pl.semaphore_signal(tokens.at[index], inc=1, device_id=(at(step), s), device_id_type=MESH)

    token(0)

    loads[1].wait()
    bt[...] = bv[...].T
    for h in range(2):
        loads[0 if h == 0 else 2].wait()

        @pl.when(s < slabs - 1)
        def _():
            left = mm(bt[...], gv[h]).astype(BF16)
            low_out[h] = mm(left, bv[...]).astype(BF16)
            ups[h].start()

    pl.semaphore_wait(tokens.at[0], len(near))
    token(1)

    @pl.when(s < slabs - 1)
    def _():
        for h in range(2):
            downs[h].wait_recv()
            left = mm(bv[...], gup[h]).astype(BF16)
            couple[h] = mm(left, bt[...]).astype(BF16)

    @pl.when(last)
    def _():
        couple[...] = jnp.zeros_like(couple)

    pl.semaphore_wait(tokens.at[1], len(near))
    token(2)

    @pl.when(s > 0)
    def _():
        for h in range(2):
            ups[h].wait_recv()
            couple[h] = (couple[h].astype(F32) + low_in[h].astype(F32)).astype(BF16)

    pl.semaphore_wait(tokens.at[2], len(near))

    sends = {}

    def send(h, a, b, c):
        rows = pl.ds(c * ROWS, ROWS)
        source = greens.at[h, rows] if a == 0 else slots.at[slot_of(a), h, rows]
        index = len(sends)
        copy = pltpu.make_async_remote_copy(
            src_ref=source, dst_ref=slots.at[slot_of(b), h, rows],
            send_sem=hsend.at[index], recv_sem=hrecv.at[index],
            device_id=(at(b - a), s), device_id_type=MESH)
        copy.start()
        sends[(h, b, c)] = copy

    got = set()

    def arrived(h, o, c):
        if o != 0 and (h, o, c) not in got:
            got.add((h, o, c))
            sends[(h, o, c)].wait_recv()

    steps = plan(distances)
    early = [step for step in steps if step[0] == "send" and step[2] == 0]
    inv = 1.0 / M
    for c in range(CHUNKS):
        rows = pl.ds(c * ROWS, ROWS)
        gr, gi = gv[0, rows], gv[1, rows]
        dr = (mm(gr, couple[0]) - mm(gi, couple[1])).astype(BF16)
        di = (mm(gr, couple[1]) + mm(gi, couple[0])).astype(BF16)
        outr = mm(dr, gv[0]) - mm(di, gv[1])
        greens[0, rows] = (gr.astype(F32) + outr * inv).astype(BF16)
        outi = mm(dr, gv[1]) + mm(di, gv[0])
        greens[1, rows] = (gi.astype(F32) + outi * inv).astype(BF16)
        for step in early:
            if step[4] == c and (step[1], step[3]) in ((0, 1), (1, -1)):
                send(*step[1:])

    eye = lax.broadcasted_iota(jnp.int32, (128, 128), 0) == lax.broadcasted_iota(jnp.int32, (128, 128), 1)
    position = (e.astype(F32) + 0.5 - energies / 2) * 4.0 / energies
    holes = 1.0 / (1.0 + jnp.exp(-jnp.full((1, 128), position, F32)))
    for b in range(M // 128):
        block = greens[1, pl.ds(b * 128, 128), pl.ds(b * 128, 128)].astype(F32)
        diag = jnp.sum(jnp.where(eye, block, 0.0), axis=0, keepdims=True)
        own_sum[:, pl.ds(b * 128, 128)] = -holes * diag

    small = {}

    def small_send(name, index, source, target, step):
        copy = pltpu.make_async_remote_copy(
            src_ref=source, dst_ref=target, send_sem=ssend.at[index], recv_sem=srecv.at[index],
            device_id=(at(step), s), device_id_type=MESH)
        copy.start()
        small[(name, index)] = copy

    for j in range(3):
        small_send("one", j, own_sum, got1.at[j], j + 1)

    def take(name, base, count, stride, got_ref, value):
        for j in range(count):
            small[(name, base + j)].wait_recv()
            keep = jnp.where(e >= (j + 1) * stride, 1.0, 0.0)
            value = value + got_ref[j] * keep
        return value

    def sum4():
        own4[...] = take("one", 0, 3, 1, got1, own_sum[...])
        small_send("four", 3, own4, got4.at[0], 4)

    def sum8():
        own8[...] = take("four", 3, 1, 4, got4, own4[...])
        for j in range(3):
            small_send("eight", 4 + j, own8, got8.at[j], ROW * (j + 1))

    def sum32():
        own32[...] = take("eight", 4, 3, 8, got8, own8[...])
        small_send("rest", 7, own32, got32.at[0], 32)

    def sum64():
        cum_ref[...] = take("rest", 7, 1, 32, got32, own32[...])

    sums = {"sum4": sum4, "sum8": sum8, "sum32": sum32, "sum64": sum64}

    for k in range(MODES):
        if k == 0:
            loads[3].wait()
        pt[k] = pv[k].T

    started = []

    def product(d, h):
        for o in (d, -d):
            for c in range(CHUNKS):
                arrived(h, o, c)
        mode = jnp.int32(0)
        factor = F32(0.0)
        has = F32(0.0)
        for k in range(MODES):
            same = off_ref[k] == d
            mode = jnp.where(same, k, mode)
            factor = jnp.where(same, bose_ref[k], factor)
            has = jnp.where(same, 1.0, has)
        low = jnp.where(e >= d, (factor + 1.0) * has, 0.0)
        high = jnp.where(e < energies - d, factor * has, 0.0)
        mix = (low * slots[slot_of(d), h].astype(F32) + high * slots[slot_of(-d), h].astype(F32)).astype(BF16)
        left = mm(pv[mode], mix).astype(BF16)
        part = mm(left, pt[mode])
        if h in started:
            part = acc[h] + part
        started.append(h)
        if started.count(h) == len(distances):
            sigma_ref[0, :, pl.ds(h * M, M)] = part.astype(BF16)
        else:
            acc[h] = part

    for step in steps:
        if step[0] == "send":
            if (step[1], step[3], step[4]) in sends:
                continue
            arrived(step[1], step[2], step[4])
            send(*step[1:])
        elif step[0] == "product":
            product(*step[1:])
        else:
            sums[step[0]]()

    for copy in sends.values():
        copy.wait_send()
    for copy in small.values():
        copy.wait_send()

    @pl.when(s > 0)
    def _():
        for copy in downs:
            copy.wait_send()

    @pl.when(s < slabs - 1)
    def _():
        for copy in ups:
            copy.wait_send()


def body(green_local, coupling, phonon_coupling, offsets, bose_factors, distances):
    energies = lax.axis_size("energy")
    slabs = lax.axis_size("slab")
    any_spec = pl.BlockSpec(memory_space=pl.ANY)
    smem_spec = pl.BlockSpec(memory_space=pltpu.SMEM)
    vmem_spec = pl.BlockSpec(memory_space=pltpu.VMEM)
    hops = CHUNKS * 2 * sum(len(routes) for routes in ROUTES[distances].values())
    half = (M, M)
    return pl.pallas_call(
        functools.partial(kernel, distances, energies, slabs),
        out_shape=(
            jax.ShapeDtypeStruct((1, M, 2 * M), BF16),
            jax.ShapeDtypeStruct((1, M), F32),
        ),
        in_specs=[any_spec, any_spec, any_spec, smem_spec, smem_spec],
        out_specs=(vmem_spec, vmem_spec),
        scratch_shapes=[
            pltpu.VMEM((2, *half), BF16),
            pltpu.VMEM(half, BF16),
            pltpu.VMEM(half, BF16),
            pltpu.VMEM((MODES, *half), BF16),
            pltpu.VMEM((MODES, *half), BF16),
            pltpu.VMEM((2, *half), BF16),
            pltpu.VMEM((2, *half), BF16),
            pltpu.VMEM((2, *half), BF16),
            pltpu.VMEM((2, *half), BF16),
            pltpu.VMEM((2, *half), BF16),
            pltpu.VMEM((8, 2, *half), BF16),
            pltpu.VMEM((2, *half), F32),
            pltpu.VMEM((1, M), F32),
            pltpu.VMEM((1, M), F32),
            pltpu.VMEM((1, M), F32),
            pltpu.VMEM((1, M), F32),
            pltpu.VMEM((3, 1, M), F32),
            pltpu.VMEM((1, 1, M), F32),
            pltpu.VMEM((3, 1, M), F32),
            pltpu.VMEM((1, 1, M), F32),
            pltpu.SemaphoreType.DMA((4,)),
            pltpu.SemaphoreType.DMA((4,)),
            pltpu.SemaphoreType.DMA((4,)),
            pltpu.SemaphoreType.DMA((hops,)),
            pltpu.SemaphoreType.DMA((hops,)),
            pltpu.SemaphoreType.DMA((8,)),
            pltpu.SemaphoreType.DMA((8,)),
            pltpu.SemaphoreType.REGULAR((3,)),
        ],
        compiler_params=pltpu.CompilerParams(collective_id=0, has_side_effects=True),
    )(green_local, coupling, phonon_coupling, offsets, bose_factors)


def solution(mesh):
    in_specs = (P("energy", "slab", None), P("slab", None), P(), P(), P())
    out_specs = (P("energy", "slab", None), P("energy", "slab"))
    run = functools.partial(body, distances=(1, 2, 3, 4))
    return jax.shard_map(run, mesh=mesh, in_specs=in_specs, out_specs=out_specs, check_vma=False)
```

```python
import functools

import jax
import jax.numpy as jnp
from jax import lax
from jax.experimental import pallas as pl
from jax.experimental.pallas import tpu as pltpu
from jax.sharding import PartitionSpec as P

M = 384
MODES = 3
ROW = 8
CHUNKS = 4
ROWS = M // CHUNKS
PARTS = 2
MESH = pl.DeviceIdType.MESH
F32 = jnp.float32
BF16 = jnp.bfloat16

ROUTES = {
    (1, 2, 4): [[(0, 0, 1, 1)], [(0, 1, 2, 1)], [(0, 2, 4, 2)], [(1, 0, 1, 1)], [(1, 1, 2, 1)]],
    (1, 3, 4): [[(0, 0, 1, 1)], [(0, 1, 3, 2), (1, 0, 1, 1)], [(0, 3, 4, 1)], [(0, 4, -3, 1)]],
    (2, 3, 4): [[(0, 0, 2, 2)], [(0, 2, 3, 1)], [(0, 3, 4, 1)], [(0, 4, -3, 1)], [(0, -3, -2, 1)]],
}


def slot_of(place):
    return 3 if abs(place) == 4 else place - 1 if place > 0 else 3 - place


def lifted_slot(distance):
    return 6 + distance


def links_of(distances):
    right = ROUTES[distances]
    return {"right": right, "left": [[(1 - h, -a, -b, -step) for h, a, b, step in group] for group in right]}


def plan(distances, chunk_us=1.6, latency_us=1.6, slack_us=2.0):
    ready = {(h, 0, c): 0.8 * (c * PARTS // CHUNKS) for h in range(2) for c in range(CHUNKS)}
    links = links_of(distances)
    queues = {name: [(*route, c) for group in groups for c in range(CHUNKS) for route in group] for name, groups in links.items()}
    free = {name: 0.0 for name in links}
    last = {name: 0.0 for name in links}
    events = []
    while any(queues.values()):
        for name, queue in queues.items():
            while queue and (queue[0][0], queue[0][1], queue[0][4]) in ready:
                h, a, b, step, c = queue.pop(0)
                last[name] = max(last[name], ready[(h, a, c)])
                free[name] = max(free[name], ready[(h, a, c)]) + 2 * chunk_us * abs(step)
                ready[(h, b, c)] = free[name] + latency_us
                events.append((last[name], 0, ("send", h, a, b, step, c)))
    lifts = []
    for (h, b, c), when in ready.items():
        if abs(b) == 4:
            lifts.append((when, ("lift", h, b, 4, c)))
            lifts.append((when, ("lift", h, b, -4, c)))
        elif b != 0:
            lifts.append((when, ("lift", h, b, b, c)))
    lifts.sort()
    busy = {1: 0.0, -1: 0.0}
    done = {}
    for when, lift in lifts:
        events.append((when, 1, lift))
        way = 1 if lift[3] > 0 else -1
        busy[way] = max(busy[way], when) + 2 * chunk_us
        done[abs(lift[3])] = max(done.get(abs(lift[3]), 0.0), busy[way] + latency_us)
    for d in distances:
        events.append((done[d] + slack_us, 2, ("product", d)))
    for order, name in enumerate(("sum4", "sum8", "sum32", "sum64")):
        events.append((9.0 + 7.5 * order, 3, (name,)))
    events.sort(key=lambda event: event[:2])
    return [event[2] for event in events]


def mm(a, b):
    return jnp.dot(a, b, preferred_element_type=F32)


def kernel(
    distances, energies, slabs,
    g_hbm, b_hbm, p_hbm, off_ref, bose_ref,
    sigma_ref, cum_ref,
    gv, bv, bt, pv, pt, gup, low_in, low_out, couple, greens, slots, acc,
    own_sum, own4, own8, own32, got1, got4, got8, got32,
    load_sem, zsend, zrecv, hsend, hrecv, ysend, yrecv, ssend, srecv, tokens,
):
    e = lax.axis_index("energy")
    s = lax.axis_index("slab")
    first = s == 0
    last = s == slabs - 1

    def at(step):
        return lax.rem(e + (step + energies), energies)

    column = lax.rem(e, ROW)

    def along(step):
        return e - column + lax.rem(column + (step + ROW), ROW)

    near = (along(1), along(-1), at(ROW), at(-ROW))
    barrier = pltpu.get_barrier_semaphore()
    for device in near:
        pl.semaphore_signal(barrier, inc=1, device_id=(device, s), device_id_type=MESH)

    @pl.when(s > 0)
    def _():
        pl.semaphore_signal(barrier, inc=1, device_id=(e, s - 1), device_id_type=MESH)

    @pl.when(s < slabs - 1)
    def _():
        pl.semaphore_signal(barrier, inc=1, device_id=(e, s + 1), device_id_type=MESH)

    loads = [
        pltpu.make_async_copy(g_hbm.at[0, :, pl.ds(0, M)], gv.at[0], load_sem.at[0]),
        pltpu.make_async_copy(b_hbm, bv, load_sem.at[1]),
        pltpu.make_async_copy(g_hbm.at[0, :, pl.ds(M, M)], gv.at[1], load_sem.at[2]),
        pltpu.make_async_copy(p_hbm, pv, load_sem.at[3]),
    ]
    for load in loads:
        load.start()

    slab_links = jnp.where(first, 0, 1) + jnp.where(last, 0, 1)
    pl.semaphore_wait(barrier, len(near) + slab_links)

    def down(h):
        return pltpu.make_async_remote_copy(
            src_ref=g_hbm.at[0, :, pl.ds(h * M, M)], dst_ref=gup.at[h],
            send_sem=zsend.at[h], recv_sem=zrecv.at[h],
            device_id=(e, s - 1), device_id_type=MESH)

    def up(h):
        return pltpu.make_async_remote_copy(
            src_ref=low_out.at[h], dst_ref=low_in.at[h],
            send_sem=zsend.at[2 + h], recv_sem=zrecv.at[2 + h],
            device_id=(e, s + 1), device_id_type=MESH)

    @pl.when(s > 0)
    def _():
        for h in range(2):
            down(h).start()

    def token(index):
        for device in near:
            pl.semaphore_signal(tokens.at[index], inc=1, device_id=(device, s), device_id_type=MESH)

    token(0)

    loads[1].wait()
    bt[...] = bv[...].T
    loads[0].wait()
    loads[2].wait()

    @pl.when(s < slabs - 1)
    def _():
        @pl.loop(0, 2)
        def _(h):
            left = mm(bt[...], gv[h]).astype(BF16)
            low_out[h] = mm(left, bv[...]).astype(BF16)
            up(h).start()

    pl.semaphore_wait(tokens.at[0], len(near))
    token(1)

    @pl.when(s < slabs - 1)
    def _():
        @pl.loop(0, 2)
        def _(h):
            for side in range(2):
                @pl.when(h == side)
                def _():
                    down(side).wait_recv()
            left = mm(bv[...], gup[h]).astype(BF16)
            couple[h] = mm(left, bt[...]).astype(BF16)

    @pl.when(last)
    def _():
        couple[...] = jnp.zeros_like(couple)

    pl.semaphore_wait(tokens.at[1], len(near))
    token(2)

    @pl.when(s > 0)
    def _():
        for h in range(2):
            up(h).wait_recv()
            couple[h] = (couple[h].astype(F32) + low_in[h].astype(F32)).astype(BF16)

    pl.semaphore_wait(tokens.at[2], len(near))
    token(3)

    links = links_of(distances)
    routes = [route for name in links for group in links[name] for route in group]
    number = {(h, b): index for index, (h, _, b, _) in enumerate(routes)}

    def hop(h, a, b, step, c):
        rows = pl.ds(c * ROWS, ROWS)
        source = greens.at[h, rows] if a == 0 else slots.at[slot_of(a), h, rows]
        index = number[(h, b)] * CHUNKS + c
        return pltpu.make_async_remote_copy(
            src_ref=source, dst_ref=slots.at[slot_of(b), h, rows],
            send_sem=hsend.at[index], recv_sem=hrecv.at[index],
            device_id=(along(step), s), device_id_type=MESH)

    def wraps(r):
        return column < r if r > 0 else column > ROW - 1 + r

    def gives(r):
        return jnp.logical_and(wraps(r), e < energies - ROW if r > 0 else e >= ROW)

    def takes(r):
        return jnp.logical_and(wraps(r), e >= ROW if r > 0 else e < energies - ROW)

    def lift(h, b, r, c):
        rows = pl.ds(c * ROWS, ROWS)
        index = (distances.index(abs(r)) * 2 + h) * CHUNKS + c
        return pltpu.make_async_remote_copy(
            src_ref=slots.at[slot_of(b), h, rows], dst_ref=slots.at[lifted_slot(abs(r)), h, rows],
            send_sem=ysend.at[index], recv_sem=yrecv.at[index],
            device_id=(at(ROW if r > 0 else -ROW), s), device_id_type=MESH)

    origin = {(h, b): (h, a, b, step) for h, a, b, step in routes}
    got = set()

    def arrived(h, o, c):
        if o != 0 and (h, o, c) not in got:
            got.add((h, o, c))
            hop(*origin[(h, o)], c).wait_recv()

    inv = 1.0 / M
    leading = (links["right"][0][0], links["left"][0][0])
    early = CHUNKS // PARTS

    @pl.loop(0, PARTS)
    def _(part):
        rows = pl.ds(pl.multiple_of(part * (M // PARTS), 32), M // PARTS)
        gr, gi = gv[0, rows], gv[1, rows]
        dr = (mm(gr, couple[0]) - mm(gi, couple[1])).astype(BF16)
        di = (mm(gr, couple[1]) + mm(gi, couple[0])).astype(BF16)
        outr = mm(dr, gv[0]) - mm(di, gv[1])
        greens[0, rows] = (gr.astype(F32) + outr * inv).astype(BF16)
        outi = mm(dr, gv[1]) + mm(di, gv[0])
        greens[1, rows] = (gi.astype(F32) + outi * inv).astype(BF16)

        @pl.when(part == 0)
        def _():
            for c in range(early):
                for route in leading:
                    hop(*route, c).start()

    eye = lax.broadcasted_iota(jnp.int32, (128, 128), 0) == lax.broadcasted_iota(jnp.int32, (128, 128), 1)
    position = (e.astype(F32) + 0.5 - energies / 2) * 4.0 / energies
    holes = 1.0 / (1.0 + jnp.exp(-jnp.full((1, 128), position, F32)))
    for b in range(M // 128):
        block = greens[1, pl.ds(b * 128, 128), pl.ds(b * 128, 128)].astype(F32)
        diag = jnp.sum(jnp.where(eye, block, 0.0), axis=0, keepdims=True)
        own_sum[:, pl.ds(b * 128, 128)] = -holes * diag

    small = {}

    def small_send(name, index, source, target, step):
        copy = pltpu.make_async_remote_copy(
            src_ref=source, dst_ref=target, send_sem=ssend.at[index], recv_sem=srecv.at[index],
            device_id=(at(step), s), device_id_type=MESH)
        copy.start()
        small[(name, index)] = copy

    for j in range(3):
        small_send("one", j, own_sum, got1.at[j], j + 1)

    for c in range(early, CHUNKS):
        for route in leading:
            hop(*route, c).start()

    def take(name, base, count, stride, got_ref, value):
        for j in range(count):
            small[(name, base + j)].wait_recv()
            keep = jnp.where(e >= (j + 1) * stride, 1.0, 0.0)
            value = value + got_ref[j] * keep
        return value

    def sum4():
        own4[...] = take("one", 0, 3, 1, got1, own_sum[...])
        small_send("four", 3, own4, got4.at[0], 4)

    def sum8():
        own8[...] = take("four", 3, 1, 4, got4, own4[...])
        for j in range(3):
            small_send("eight", 4 + j, own8, got8.at[j], ROW * (j + 1))

    def sum32():
        own32[...] = take("eight", 4, 3, 8, got8, own8[...])
        small_send("rest", 7, own32, got32.at[0], 32)

    def sum64():
        cum_ref[...] = take("rest", 7, 1, 32, got32, own32[...])

    sums = {"sum4": sum4, "sum8": sum8, "sum32": sum32, "sum64": sum64}

    pl.semaphore_wait(tokens.at[3], len(near))
    loads[3].wait()

    @pl.loop(0, MODES)
    def _(k):
        pt[k] = pv[k].T

    done = []

    def product(d):
        for r in (d, -d):
            @pl.when(takes(r))
            def _():
                for h in range(2):
                    for c in range(CHUNKS):
                        lift(h, r, r, c).wait_recv()
        mode = jnp.int32(0)
        factor = F32(0.0)
        for k in range(MODES):
            same = off_ref[k] == d
            mode = jnp.where(same, k, mode)
            factor = jnp.where(same, bose_ref[k], factor)
        low = jnp.where(e >= d, factor + 1.0, 0.0)
        high = jnp.where(e < energies - d, factor, 0.0)
        near_low = jnp.where(takes(d), lifted_slot(d), slot_of(d))
        near_high = jnp.where(takes(-d), lifted_slot(d), slot_of(-d))
        place = len(done)
        done.append(d)

        @pl.loop(0, 2)
        def _(h):
            mix = (low * slots[near_low, h].astype(F32) + high * slots[near_high, h].astype(F32)).astype(BF16)
            left = mm(pv[mode], mix).astype(BF16)
            part = mm(left, pt[mode])
            if place > 0:
                part = acc[h] + part
            if place == len(distances) - 1:
                sigma_ref[0, :, pl.ds(pl.multiple_of(h * M, 128), M)] = part.astype(BF16)
            else:
                acc[h] = part

    for step in plan(distances):
        if step[0] == "send":
            if step[1:5] in leading:
                continue
            arrived(step[1], step[2], step[5])
            hop(*step[1:]).start()
        elif step[0] == "lift":
            arrived(step[1], step[2], step[4])

            @pl.when(gives(step[3]))
            def _():
                lift(*step[1:]).start()
        elif step[0] == "product":
            product(step[1])
        else:
            sums[step[0]]()

    for route in routes:
        for c in range(CHUNKS):
            hop(*route, c).wait_send()
    for d in distances:
        for r in (d, -d):
            @pl.when(gives(r))
            def _():
                for h in range(2):
                    for c in range(CHUNKS):
                        lift(h, r, r, c).wait_send()
    for copy in small.values():
        copy.wait_send()

    @pl.when(s > 0)
    def _():
        for h in range(2):
            down(h).wait_send()

    @pl.when(s < slabs - 1)
    def _():
        for h in range(2):
            up(h).wait_send()


def whole(distances, number, green_local, coupling, phonon_coupling, offsets, bose_factors):
    energies = lax.axis_size("energy")
    slabs = lax.axis_size("slab")
    any_spec = pl.BlockSpec(memory_space=pl.ANY)
    smem_spec = pl.BlockSpec(memory_space=pltpu.SMEM)
    vmem_spec = pl.BlockSpec(memory_space=pltpu.VMEM)
    hops = CHUNKS * sum(len(group) for groups in links_of(distances).values() for group in groups)
    half = (M, M)
    return pl.pallas_call(
        functools.partial(kernel, distances, energies, slabs),
        out_shape=(
            jax.ShapeDtypeStruct((1, M, 2 * M), BF16),
            jax.ShapeDtypeStruct((1, M), F32),
        ),
        in_specs=[any_spec, any_spec, any_spec, smem_spec, smem_spec],
        out_specs=(vmem_spec, vmem_spec),
        scratch_shapes=[
            pltpu.VMEM((2, *half), BF16),
            pltpu.VMEM(half, BF16),
            pltpu.VMEM(half, BF16),
            pltpu.VMEM((MODES, *half), BF16),
            pltpu.VMEM((MODES, *half), BF16),
            pltpu.VMEM((2, *half), BF16),
            pltpu.VMEM((2, *half), BF16),
            pltpu.VMEM((2, *half), BF16),
            pltpu.VMEM((2, *half), BF16),
            pltpu.VMEM((2, *half), BF16),
            pltpu.VMEM((11, 2, *half), BF16),
            pltpu.VMEM((2, *half), F32),
            pltpu.VMEM((1, M), F32),
            pltpu.VMEM((1, M), F32),
            pltpu.VMEM((1, M), F32),
            pltpu.VMEM((1, M), F32),
            pltpu.VMEM((3, 1, M), F32),
            pltpu.VMEM((1, 1, M), F32),
            pltpu.VMEM((3, 1, M), F32),
            pltpu.VMEM((1, 1, M), F32),
            pltpu.SemaphoreType.DMA((4,)),
            pltpu.SemaphoreType.DMA((4,)),
            pltpu.SemaphoreType.DMA((4,)),
            pltpu.SemaphoreType.DMA((hops,)),
            pltpu.SemaphoreType.DMA((hops,)),
            pltpu.SemaphoreType.DMA((2 * CHUNKS * len(distances),)),
            pltpu.SemaphoreType.DMA((2 * CHUNKS * len(distances),)),
            pltpu.SemaphoreType.DMA((8,)),
            pltpu.SemaphoreType.DMA((8,)),
            pltpu.SemaphoreType.REGULAR((4,)),
        ],
        compiler_params=pltpu.CompilerParams(collective_id=number, has_side_effects=True),
    )(green_local, coupling, phonon_coupling, offsets, bose_factors)


def body(green_local, coupling, phonon_coupling, offsets, bose_factors):
    missing = 10 - jnp.sum(offsets)
    branches = [
        functools.partial(whole, distances, number)
        for number, distances in enumerate(((2, 3, 4), (1, 3, 4), (1, 2, 4)))
    ]
    return lax.switch(missing - 1, branches, green_local, coupling, phonon_coupling, offsets, bose_factors)


def solution(mesh):
    in_specs = (P("energy", "slab", None), P("slab", None), P(), P(), P())
    out_specs = (P("energy", "slab", None), P("energy", "slab"))
    return jax.shard_map(body, mesh=mesh, in_specs=in_specs, out_specs=out_specs, check_vma=False)
```

```python
import functools

import jax
import jax.numpy as jnp
from jax import lax
from jax.experimental import pallas as pl
from jax.experimental.pallas import tpu as pltpu
from jax.sharding import PartitionSpec as P

M = 384
MODES = 3
ROW = 8
CHUNKS = 4
ROWS = M // CHUNKS
PARTS = 2
MESH = pl.DeviceIdType.MESH
F32 = jnp.float32
BF16 = jnp.bfloat16

ROUTES = {
    (1, 2, 4): [[(0, 0, 1, 1)], [(0, 1, 2, 1)], [(0, 2, 4, 2)], [(1, 0, 1, 1)], [(1, 1, 2, 1)]],
    (1, 3, 4): [[(0, 0, 1, 1)], [(0, 1, 3, 2), (1, 0, 1, 1)], [(0, 3, 4, 1)], [(0, 4, -3, 1)]],
    (2, 3, 4): [[(0, 0, 2, 2)], [(0, 2, 3, 1)], [(0, 3, 4, 1)], [(0, 4, -3, 1)], [(0, -3, -2, 1)]],
}


def slot_of(place):
    return 3 if abs(place) == 4 else place - 1 if place > 0 else 3 - place


def lifted_slot(distance):
    return 6 + distance


def links_of(distances):
    right = ROUTES[distances]
    return {"right": right, "left": [[(1 - h, -a, -b, -step) for h, a, b, step in group] for group in right]}


def crosses(route):
    return abs(route[1]) == 4 and route[1] * route[2] < 0


def width(distances, h, r):
    groups = sum(links_of(distances).values(), [])
    turned = [(half, b) for group in groups for half, _, b, step in group if b * step < 0]
    if (h, r) not in turned:
        return abs(r)
    return int((1 - h, -2 if r > 0 else 2) in [(1 - half, -b) for half, b in turned] and abs(r) == 3)


def plan(distances, chunk_us=1.6, latency_us=1.6, slack_us=2.0):
    ready = {(h, 0, c): 0.8 * (c * PARTS // CHUNKS) for h in range(2) for c in range(CHUNKS)}
    links = links_of(distances)
    queues = {name: [(*route, c) for group in groups for c in range(CHUNKS) for route in group] for name, groups in links.items()}
    free = {name: 0.0 for name in links}
    last = {name: 0.0 for name in links}
    events = []
    while any(queues.values()):
        for name, queue in queues.items():
            while queue and (queue[0][0], queue[0][1], queue[0][4]) in ready:
                h, a, b, step, c = queue.pop(0)
                source = ready[(h, a, c)] + (3.2 if crosses((h, a, b, step)) else 0.0)
                last[name] = max(last[name], source)
                free[name] = max(free[name], source) + 2 * chunk_us * abs(step)
                ready[(h, b, c)] = free[name] + latency_us
                events.append((last[name], 0, ("send", h, a, b, step, c)))
    lifts = []
    for (h, b, c), when in ready.items():
        if abs(b) == 4:
            lifts.append((when, ("lift", h, b, 4, c)))
            lifts.append((when, ("lift", h, b, -4, c)))
        elif b != 0:
            lifts.append((when, ("lift", h, b, b, c)))
    lifts.sort()
    busy = {1: 0.0, -1: 0.0}
    done = {}
    for when, lift in lifts:
        if width(distances, lift[1], lift[3]) == 0:
            done[abs(lift[3])] = max(done.get(abs(lift[3]), 0.0), when)
            continue
        stays = abs(lift[3]) == 4 and lift[2] == lift[3] and distances != (1, 2, 4)
        events.append((when + (4.0 if stays else 0.0), 1, lift))
        way = 1 if lift[3] > 0 else -1
        busy[way] = max(busy[way], when) + 2 * chunk_us
        done[abs(lift[3])] = max(done.get(abs(lift[3]), 0.0), busy[way] + latency_us)
    for d in distances:
        events.append((done[d] + slack_us, 2, ("product", d)))
    for order, name in enumerate(("sum4", "sum8", "sum32", "sum64")):
        events.append((9.0 + 7.5 * order, 3, (name,)))
    events.sort(key=lambda event: event[:2])
    return [event[2] for event in events]


def mm(a, b):
    return jnp.dot(a, b, preferred_element_type=F32)


def kernel(
    distances, energies, slabs,
    g_hbm, b_hbm, p_hbm, off_ref, bose_ref,
    sigma_ref, cum_ref,
    gv, bv, bt, pv, pt, gup, low_in, low_out, couple, greens, slots, acc,
    own_sum, own4, own8, own32, got1, got4, got8, got32,
    load_sem, zsend, zrecv, hsend, hrecv, ysend, yrecv, ssend, srecv, tokens,
):
    e = lax.axis_index("energy")
    s = lax.axis_index("slab")
    first = s == 0
    last = s == slabs - 1

    def at(step):
        return lax.rem(e + (step + energies), energies)

    column = lax.rem(e, ROW)

    def along(step):
        return e - column + lax.rem(column + (step + ROW), ROW)

    near = (along(1), along(-1), at(ROW), at(-ROW))
    barrier = pltpu.get_barrier_semaphore()
    for device in near:
        pl.semaphore_signal(barrier, inc=1, device_id=(device, s), device_id_type=MESH)

    @pl.when(s > 0)
    def _():
        pl.semaphore_signal(barrier, inc=1, device_id=(e, s - 1), device_id_type=MESH)

    @pl.when(s < slabs - 1)
    def _():
        pl.semaphore_signal(barrier, inc=1, device_id=(e, s + 1), device_id_type=MESH)

    loads = [
        pltpu.make_async_copy(g_hbm.at[0, :, pl.ds(0, M)], gv.at[0], load_sem.at[0]),
        pltpu.make_async_copy(b_hbm, bv, load_sem.at[1]),
        pltpu.make_async_copy(g_hbm.at[0, :, pl.ds(M, M)], gv.at[1], load_sem.at[2]),
        pltpu.make_async_copy(p_hbm, pv, load_sem.at[3]),
    ]
    for load in loads:
        load.start()

    slab_links = jnp.where(first, 0, 1) + jnp.where(last, 0, 1)
    pl.semaphore_wait(barrier, len(near) + slab_links)

    def down(h):
        return pltpu.make_async_remote_copy(
            src_ref=g_hbm.at[0, :, pl.ds(h * M, M)], dst_ref=gup.at[h],
            send_sem=zsend.at[h], recv_sem=zrecv.at[h],
            device_id=(e, s - 1), device_id_type=MESH)

    def up(h):
        return pltpu.make_async_remote_copy(
            src_ref=low_out.at[h], dst_ref=low_in.at[h],
            send_sem=zsend.at[2 + h], recv_sem=zrecv.at[2 + h],
            device_id=(e, s + 1), device_id_type=MESH)

    @pl.when(s > 0)
    def _():
        for h in range(2):
            down(h).start()

    def token(index):
        for device in near:
            pl.semaphore_signal(tokens.at[index], inc=1, device_id=(device, s), device_id_type=MESH)

    token(0)

    loads[1].wait()
    bt[...] = bv[...].T
    loads[0].wait()
    loads[2].wait()

    @pl.when(s < slabs - 1)
    def _():
        @pl.loop(0, 2)
        def _(h):
            left = mm(bt[...], gv[h]).astype(BF16)
            low_out[h] = mm(left, bv[...]).astype(BF16)
            up(h).start()

    pl.semaphore_wait(tokens.at[0], len(near))
    token(1)

    @pl.when(s < slabs - 1)
    def _():
        @pl.loop(0, 2)
        def _(h):
            for side in range(2):
                @pl.when(h == side)
                def _():
                    down(side).wait_recv()
            left = mm(bv[...], gup[h]).astype(BF16)
            couple[h] = mm(left, bt[...]).astype(BF16)

    @pl.when(last)
    def _():
        couple[...] = jnp.zeros_like(couple)

    pl.semaphore_wait(tokens.at[1], len(near))
    token(2)

    @pl.when(s > 0)
    def _():
        for h in range(2):
            up(h).wait_recv()
            couple[h] = (couple[h].astype(F32) + low_in[h].astype(F32)).astype(BF16)

    pl.semaphore_wait(tokens.at[2], len(near))
    token(3)

    links = links_of(distances)
    routes = [route for name in links for group in links[name] for route in group]
    number = {(h, b): index for index, (h, _, b, _) in enumerate(routes)}

    def ends(r, count):
        return column < count if r > 0 else column > ROW - 1 - count

    def gives(h, r):
        return jnp.logical_and(ends(r, width(distances, h, r)), e < energies - ROW if r > 0 else e >= ROW)

    def takes(h, r):
        return jnp.logical_and(ends(r, width(distances, h, r)), e >= ROW if r > 0 else e < energies - ROW)

    def turns(h, b):
        r = 4 if b > 0 else -4
        return jnp.logical_and(takes(h, r), jnp.logical_not(ends(r, width(distances, h, b) + 1)))

    def hop(h, a, b, step, c):
        rows = pl.ds(c * ROWS, ROWS)
        if crosses((h, a, b, step)):
            source = slots.at[jnp.where(turns(h, b), lifted_slot(4), slot_of(4)), h, rows]
        else:
            source = greens.at[h, rows] if a == 0 else slots.at[slot_of(a), h, rows]
        index = number[(h, b)] * CHUNKS + c
        return pltpu.make_async_remote_copy(
            src_ref=source, dst_ref=slots.at[slot_of(b), h, rows],
            send_sem=hsend.at[index], recv_sem=hrecv.at[index],
            device_id=(along(step), s), device_id_type=MESH)

    def lift(h, b, r, c):
        rows = pl.ds(c * ROWS, ROWS)
        index = (distances.index(abs(r)) * 2 + h) * CHUNKS + c
        return pltpu.make_async_remote_copy(
            src_ref=slots.at[slot_of(b), h, rows], dst_ref=slots.at[lifted_slot(abs(r)), h, rows],
            send_sem=ysend.at[index], recv_sem=yrecv.at[index],
            device_id=(at(ROW if r > 0 else -ROW), s), device_id_type=MESH)

    origin = {(h, b): (h, a, b, step) for h, a, b, step in routes}
    got = set()

    def arrived(h, o, c):
        if o != 0 and (h, o, c) not in got:
            got.add((h, o, c))
            hop(*origin[(h, o)], c).wait_recv()

    inv = 1.0 / M
    leading = (links["right"][0][0], links["left"][0][0])
    early = CHUNKS // PARTS

    @pl.loop(0, PARTS)
    def _(part):
        rows = pl.ds(pl.multiple_of(part * (M // PARTS), 32), M // PARTS)
        gr, gi = gv[0, rows], gv[1, rows]
        dr = (mm(gr, couple[0]) - mm(gi, couple[1])).astype(BF16)
        di = (mm(gr, couple[1]) + mm(gi, couple[0])).astype(BF16)
        outr = mm(dr, gv[0]) - mm(di, gv[1])
        greens[0, rows] = (gr.astype(F32) + outr * inv).astype(BF16)
        outi = mm(dr, gv[1]) + mm(di, gv[0])
        greens[1, rows] = (gi.astype(F32) + outi * inv).astype(BF16)

        @pl.when(part == 0)
        def _():
            for c in range(early):
                for route in leading:
                    hop(*route, c).start()

    eye = lax.broadcasted_iota(jnp.int32, (128, 128), 0) == lax.broadcasted_iota(jnp.int32, (128, 128), 1)
    position = (e.astype(F32) + 0.5 - energies / 2) * 4.0 / energies
    holes = 1.0 / (1.0 + jnp.exp(-jnp.full((1, 128), position, F32)))
    for b in range(M // 128):
        block = greens[1, pl.ds(b * 128, 128), pl.ds(b * 128, 128)].astype(F32)
        diag = jnp.sum(jnp.where(eye, block, 0.0), axis=0, keepdims=True)
        own_sum[:, pl.ds(b * 128, 128)] = -holes * diag

    small = {}

    def small_send(name, index, source, target, step):
        copy = pltpu.make_async_remote_copy(
            src_ref=source, dst_ref=target, send_sem=ssend.at[index], recv_sem=srecv.at[index],
            device_id=(at(step), s), device_id_type=MESH)
        copy.start()
        small[(name, index)] = copy

    for j in range(3):
        small_send("one", j, own_sum, got1.at[j], j + 1)

    for c in range(early, CHUNKS):
        for route in leading:
            hop(*route, c).start()

    def take(name, base, count, stride, got_ref, value):
        for j in range(count):
            small[(name, base + j)].wait_recv()
            keep = jnp.where(e >= (j + 1) * stride, 1.0, 0.0)
            value = value + got_ref[j] * keep
        return value

    def sum4():
        own4[...] = take("one", 0, 3, 1, got1, own_sum[...])
        small_send("four", 3, own4, got4.at[0], 4)

    def sum8():
        own8[...] = take("four", 3, 1, 4, got4, own4[...])
        for j in range(3):
            small_send("eight", 4 + j, own8, got8.at[j], ROW * (j + 1))

    def sum32():
        own32[...] = take("eight", 4, 3, 8, got8, own8[...])
        small_send("rest", 7, own32, got32.at[0], 32)

    def sum64():
        cum_ref[...] = take("rest", 7, 1, 32, got32, own32[...])

    sums = {"sum4": sum4, "sum8": sum8, "sum32": sum32, "sum64": sum64}

    pl.semaphore_wait(tokens.at[3], len(near))
    loads[3].wait()

    @pl.loop(0, MODES)
    def _(k):
        pt[k] = pv[k].T

    done = []

    def product(d):
        for h in range(2):
            for r in (d, -d):
                for c in range(CHUNKS):
                    if (h, r) in origin:
                        arrived(h, r, c)
        for r in (d, -d):
            for h in range(2):
                if width(distances, h, r) == 0:
                    continue
                waits = takes(h, r)
                for route in routes:
                    if d == 4 and route[0] == h and crosses(route) and route[2] * r > 0:
                        waits = jnp.logical_and(waits, jnp.logical_not(turns(h, route[2])))

                @pl.when(waits)
                def _():
                    for c in range(CHUNKS):
                        lift(h, r, r, c).wait_recv()
        mode = jnp.int32(0)
        factor = F32(0.0)
        for k in range(MODES):
            same = off_ref[k] == d
            mode = jnp.where(same, k, mode)
            factor = jnp.where(same, bose_ref[k], factor)
        low = jnp.where(e >= d, factor + 1.0, 0.0)
        high = jnp.where(e < energies - d, factor, 0.0)
        near_low = [jnp.where(takes(h, d), lifted_slot(d), slot_of(d)) for h in range(2)]
        near_high = [jnp.where(takes(h, -d), lifted_slot(d), slot_of(-d)) for h in range(2)]
        place = len(done)
        done.append(d)

        @pl.loop(0, 2)
        def _(h):
            below = jnp.where(h == 0, near_low[0], near_low[1])
            above = jnp.where(h == 0, near_high[0], near_high[1])
            mix = (low * slots[below, h].astype(F32) + high * slots[above, h].astype(F32)).astype(BF16)
            left = mm(pv[mode], mix).astype(BF16)
            part = mm(left, pt[mode])
            if place > 0:
                part = acc[h] + part
            if place == len(distances) - 1:
                sigma_ref[0, :, pl.ds(pl.multiple_of(h * M, 128), M)] = part.astype(BF16)
            else:
                acc[h] = part

    for step in plan(distances):
        if step[0] == "send":
            if step[1:5] in leading:
                continue
            arrived(step[1], step[2], step[5])
            if crosses(step[1:]):
                @pl.when(turns(step[1], step[3]))
                def _():
                    r = 4 if step[3] > 0 else -4
                    lift(step[1], step[2], r, step[5]).wait_recv()
            hop(*step[1:]).start()
        elif step[0] == "lift":
            arrived(step[1], step[2], step[4])

            @pl.when(gives(step[1], step[3]))
            def _():
                lift(*step[1:]).start()
        elif step[0] == "product":
            product(step[1])
        else:
            sums[step[0]]()

    for route in routes:
        for c in range(CHUNKS):
            hop(*route, c).wait_send()
    for d in distances:
        for r in (d, -d):
            for h in range(2):
                if width(distances, h, r) == 0:
                    continue

                @pl.when(gives(h, r))
                def _():
                    for c in range(CHUNKS):
                        lift(h, r, r, c).wait_send()
    for copy in small.values():
        copy.wait_send()

    @pl.when(s > 0)
    def _():
        for h in range(2):
            down(h).wait_send()

    @pl.when(s < slabs - 1)
    def _():
        for h in range(2):
            up(h).wait_send()


def whole(distances, number, green_local, coupling, phonon_coupling, offsets, bose_factors):
    energies = lax.axis_size("energy")
    slabs = lax.axis_size("slab")
    any_spec = pl.BlockSpec(memory_space=pl.ANY)
    smem_spec = pl.BlockSpec(memory_space=pltpu.SMEM)
    vmem_spec = pl.BlockSpec(memory_space=pltpu.VMEM)
    hops = CHUNKS * sum(len(group) for groups in links_of(distances).values() for group in groups)
    half = (M, M)
    return pl.pallas_call(
        functools.partial(kernel, distances, energies, slabs),
        out_shape=(
            jax.ShapeDtypeStruct((1, M, 2 * M), BF16),
            jax.ShapeDtypeStruct((1, M), F32),
        ),
        in_specs=[any_spec, any_spec, any_spec, smem_spec, smem_spec],
        out_specs=(vmem_spec, vmem_spec),
        scratch_shapes=[
            pltpu.VMEM((2, *half), BF16),
            pltpu.VMEM(half, BF16),
            pltpu.VMEM(half, BF16),
            pltpu.VMEM((MODES, *half), BF16),
            pltpu.VMEM((MODES, *half), BF16),
            pltpu.VMEM((2, *half), BF16),
            pltpu.VMEM((2, *half), BF16),
            pltpu.VMEM((2, *half), BF16),
            pltpu.VMEM((2, *half), BF16),
            pltpu.VMEM((2, *half), BF16),
            pltpu.VMEM((11, 2, *half), BF16),
            pltpu.VMEM((2, *half), F32),
            pltpu.VMEM((1, M), F32),
            pltpu.VMEM((1, M), F32),
            pltpu.VMEM((1, M), F32),
            pltpu.VMEM((1, M), F32),
            pltpu.VMEM((3, 1, M), F32),
            pltpu.VMEM((1, 1, M), F32),
            pltpu.VMEM((3, 1, M), F32),
            pltpu.VMEM((1, 1, M), F32),
            pltpu.SemaphoreType.DMA((4,)),
            pltpu.SemaphoreType.DMA((4,)),
            pltpu.SemaphoreType.DMA((4,)),
            pltpu.SemaphoreType.DMA((hops,)),
            pltpu.SemaphoreType.DMA((hops,)),
            pltpu.SemaphoreType.DMA((2 * CHUNKS * len(distances),)),
            pltpu.SemaphoreType.DMA((2 * CHUNKS * len(distances),)),
            pltpu.SemaphoreType.DMA((8,)),
            pltpu.SemaphoreType.DMA((8,)),
            pltpu.SemaphoreType.REGULAR((4,)),
        ],
        compiler_params=pltpu.CompilerParams(collective_id=number, has_side_effects=True),
    )(green_local, coupling, phonon_coupling, offsets, bose_factors)


def body(green_local, coupling, phonon_coupling, offsets, bose_factors):
    missing = 10 - jnp.sum(offsets)
    branches = [
        functools.partial(whole, distances, number)
        for number, distances in enumerate(((2, 3, 4), (1, 3, 4), (1, 2, 4)))
    ]
    return lax.switch(missing - 1, branches, green_local, coupling, phonon_coupling, offsets, bose_factors)


def solution(mesh):
    in_specs = (P("energy", "slab", None), P("slab", None), P(), P(), P())
    out_specs = (P("energy", "slab", None), P("energy", "slab"))
    return jax.shard_map(body, mesh=mesh, in_specs=in_specs, out_specs=out_specs, check_vma=False)
```
